256 devices in a mesh: obs: 4 (over x), bfly: 64 (over z, y, core).
Axes of the slice: x: 4, y: 4, z: 8, core: 2. Of those that a mesh axis runs over, the one named last changes fastest.
Arguments:
- obs_field: float32 [262144, 1024], P(('obs', 'bfly')), may hold values from -6 to 6
- observer_leaf_bases: float32 [512, 512, 256], P(('obs', 'bfly')), may hold values from -0.25 to 0.25
- transfer: float32 [4, 512, 256, 512], P(None, ('obs', 'bfly')), may hold values from -0.25 to 0.25
- src_basis: float32 [128, 512, 256], P('bfly'), may hold values from -0.375 to 0.375
- leaf_map: int32 [4, 64], replicated, may hold values from 0 to 3, as said below
- partner_perm: int32 [4, 256], replicated, may hold values from 0 to 255, each once within a row
Outputs:
- src_field: float32 [1024, 65536], P('obs', 'bfly')
The draws below stay inside these ranges and needn't reach their ends.
Inputs may be any that keep to these rules, and one draw needn't show every extreme that they name: In every column b, leaf_map[o, b] = (o + r_b) mod 4 for one offset r_b of that column, so each column names every observer group once. `partner_perm`: each row is a permutation of the rank indices.
All inputs are finite; a program needn't handle non-finite values.
Results may differ from the reference program's by a relative error of at most 0.0001.
Values sent between devices are 32-bit elements; how exact they have to be, the bound alone decides.
No kernel may reach another device: no remote copies, remote signals or barrier semaphores. Data moves between devices by JAX's collectives and lax.ppermute only.
A program may use at most 64 MiB of HBM per device.

```python
import jax
import jax.numpy as jnp
from jax import lax

LEAF = 512
RANK = 256
COLS = 1024
NODES_DEV = 2
LEVELS = 4
OBS_NODES = 512
SRC_NODES = 128
ROWS = 262144
N_OBS = 4
N_BFLY = 64


def draw_leaf_map(key, part):
    offsets = jax.random.randint(key, (N_BFLY,), 0, N_OBS, dtype=jnp.int32)
    group_index = jnp.arange(N_OBS, dtype=jnp.int32)
    return (group_index[:, None] + offsets[None, :]) % N_OBS


def steps_of(own_key, extent, shards, smallest, top_value):
    gain = 1.0
    for position, parts in shards:
        steps = jax.random.uniform(jax.random.fold_in(jax.random.fold_in(own_key, 6), position), (parts,), jnp.float32, smallest / len(shards), top_value / len(shards))
        gain = gain * jnp.repeat(jnp.exp(steps), extent[position] // parts).reshape((-1,) + (1,) * (len(extent) - 1 - position))
    return gain


def noise(own_key, extent, width, most, cuts=(), held_as=jnp.bfloat16):
    values = jax.random.normal(own_key, extent, jnp.float32) * width
    if len(cuts) > 0:
        values = steps_of(own_key, extent, cuts, -0.22, 0.18) * values
    return jnp.clip(values, min=-most, max=most).astype(held_as)


def setup_inputs(seed: int = 0) -> dict:
    streams_of = jax.random.split(jax.random.key(seed), 7)
    obs_field = noise(streams_of[0], (ROWS, COLS), 1.0, 6.0, ((0, 256),), jnp.float32)
    observer_leaf_bases = noise(streams_of[1], (OBS_NODES, LEAF, RANK), LEAF ** -0.5, 0.25, ((0, 256),), jnp.float32)
    transfer = noise(streams_of[2], (LEVELS, OBS_NODES, RANK, 2 * RANK), (2 * RANK) ** -0.5, 0.25, ((1, 256),), jnp.float32)
    src_basis = noise(streams_of[3], (SRC_NODES, LEAF, RANK), RANK ** -0.5, 0.375, ((0, 64),), jnp.float32)
    leaf_map = draw_leaf_map(jax.random.fold_in(streams_of[6], 71), 0)
    partner_perm = jax.vmap(lambda own: jax.random.permutation(own, RANK))(jax.random.split(streams_of[5], LEVELS)).reshape((LEVELS, RANK)).astype(jnp.int32)
    return {"obs_field": obs_field, "observer_leaf_bases": observer_leaf_bases, "transfer": transfer, "src_basis": src_basis, "leaf_map": leaf_map, "partner_perm": partner_perm}


def reference(obs_field, observer_leaf_bases, transfer, src_basis, leaf_map, partner_perm):
    highest_level = lax.Precision.HIGHEST
    groups = N_OBS * N_BFLY * NODES_DEV
    block_list = obs_field.reshape(groups, LEAF, COLS)
    projected_field = jnp.einsum('hft,hfm->htm', observer_leaf_bases, block_list, precision=highest_level)
    projected_field = projected_field.reshape(N_OBS, N_BFLY, NODES_DEV, RANK, COLS)
    columns = jnp.arange(N_BFLY, dtype=jnp.int32)
    carried = projected_field[leaf_map, columns[None, :]]
    transfers = transfer.reshape(LEVELS, N_OBS, N_BFLY, NODES_DEV, RANK, 2 * RANK)
    for level_index in range(LEVELS):
        partner = carried[:, columns ^ (1 << level_index)]
        partner = jnp.take(partner, partner_perm[level_index], axis=3)
        joined = jnp.concatenate([carried, partner], axis=3)
        carried = jnp.einsum('objrs,objsc->objrc', transfers[level_index], joined, precision=highest_level)
    summed = jnp.sum(carried, axis=0)
    source_basis = src_basis.reshape(N_BFLY, NODES_DEV, LEAF, RANK)
    result = jnp.einsum('bjlr,bjrc->cbjl', source_basis, summed, precision=highest_level)
    return result.reshape(COLS, N_BFLY * NODES_DEV * LEAF)
```

```python
import functools

import jax
import jax.numpy as jnp
from jax import lax
from jax.experimental import pallas as pl
from jax.experimental.pallas import tpu as pltpu
from jax.sharding import PartitionSpec as P

CHUNKS = ((0, 0, 128), (0, 128, 128), (1, 0, 128), (1, 128, 128))
ORDER = (0, 1, 2, 3, 0, 1, 0, 2, 1, 0, 3, 2, 1, 0, 3, 2, 1, 0, 3, 2, 1, 0, 3, 2, 1, 0, 3, 2, 1, 0, 3, 2, 1, 3, 2, 3)
LIMIT = 12 << 20
CHEAP = pl.CostEstimate(flops=0, transcendentals=0, bytes_accessed=0)
NT = (((1,), (1,)), ((), ()))
TN = (((0,), (0,)), ((), ()))


def flipped(block, axis, mask):
    count = lax.axis_size(axis)
    return lax.ppermute(block, axis, [(i, i ^ mask) for i in range(count)])


def halves(block):
    high = block.astype(jnp.bfloat16)
    return high, (block - high.astype(jnp.float32)).astype(jnp.bfloat16)


def dot(a, b, dims):
    return lax.dot_general(a, b, dims, preferred_element_type=jnp.float32)


def dot3(a, b, dims):
    (ah, al), (bh, bl) = a, b
    return dot(ah, bh, dims) + (dot(ah, bl, dims) + dot(al, bh, dims))


def project_kernel(block, basis, out, high, low):
    @pl.when(pl.program_id(0) == 0)
    def _():
        high[...], low[...] = halves(basis[0])

    out[...] = dot3(halves(block[...]), (high[...], low[...]), TN)


def project(obs_field, bases, node, at, width):
    nodes, leaf, rank = bases.shape
    share = obs_field.shape[1] // 4
    return pl.pallas_call(
        project_kernel,
        grid=(4,),
        in_specs=[
            pl.BlockSpec(
                (leaf, width), lambda i: (node, (3 * i) % 4 * (share // width) + at // width)
            ),
            pl.BlockSpec((1, leaf, rank), lambda i: (node, 0, 0)),
        ],
        out_specs=pl.BlockSpec((width, rank), lambda i: (i, 0)),
        out_shape=jax.ShapeDtypeStruct((4 * width, rank), jnp.float32),
        scratch_shapes=[pltpu.VMEM((leaf, rank), jnp.bfloat16)] * 2,
        compiler_params=pltpu.CompilerParams(vmem_limit_bytes=LIMIT),
        cost_estimate=CHEAP,
    )(obs_field, bases)


def prepare_kernel(first, perm, mats, high, low):
    rank = mats.shape[2]
    h, l = halves(mats[0, 0])
    row = perm[pl.ds(first + pl.program_id(0), 1), :]
    picks = lax.broadcasted_iota(jnp.int32, (rank, rank), 0)
    onehot = (row == picks).astype(jnp.bfloat16)
    dims = NT
    for out, part in ((high, h), (low, l)):
        out[0, 0, :, :rank] = part[:, :rank]
        out[0, 0, :, rank:] = dot(part[:, rank:], onehot, dims).astype(jnp.bfloat16)


def prepare(mats, perm, first):
    levels, nodes, rank, two = mats.shape
    spec = pl.BlockSpec((1, 1, rank, two), lambda k, j: (k, j, 0, 0))
    return pl.pallas_call(
        functools.partial(prepare_kernel, first),
        grid=(levels, nodes),
        in_specs=[pl.BlockSpec(perm.shape, lambda k, j: (0, 0)), spec],
        out_specs=[spec, spec],
        out_shape=[jax.ShapeDtypeStruct(mats.shape, jnp.bfloat16)] * 2,
        compiler_params=pltpu.CompilerParams(vmem_limit_bytes=LIMIT),
        cost_estimate=CHEAP,
    )(perm, mats)


def step_kernel(a, b, high, low, out):
    rank = a.shape[1]
    h, l = high[0, 0], low[0, 0]
    out[...] = dot3(halves(a[...]), (h[:, :rank], l[:, :rank]), NT) + dot3(
        halves(b[...]), (h[:, rank:], l[:, rank:]), NT
    )


def step(a, b, mats, k, j):
    whole = pl.BlockSpec(a.shape, lambda i: (0, 0))
    one = pl.BlockSpec((1, 1) + mats[0].shape[2:], lambda i: (k, j, 0, 0))
    return pl.pallas_call(
        step_kernel,
        grid=(1,),
        in_specs=[whole, whole, one, one],
        out_specs=whole,
        out_shape=jax.ShapeDtypeStruct(a.shape, jnp.float32),
        compiler_params=pltpu.CompilerParams(vmem_limit_bytes=LIMIT),
        cost_estimate=CHEAP,
    )(a, b, *mats)


def body(obs_field, observer_leaf_bases, transfer, src_basis, leaf_map, partner_perm):
    nodes, leaf, rank = observer_leaf_bases.shape
    x = lax.axis_index("obs")
    b = lax.axis_index("bfly")

    wanted = leaf_map[x, b]
    wanted_there = leaf_map[x ^ 3, b]
    outer = jnp.where((x == 0) | (x == 3), 0, 1)
    inner = x & 1
    flags = (
        wanted_there == (x ^ 1), wanted == x, wanted == (x ^ 1),
        outer == 0, inner == 0,
    )
    flags, obs_field, transfer, partner_perm = lax.optimization_barrier(
        (flags, obs_field, transfer, partner_perm)
    )
    pass_on, stays, from_near, outer, inner = flags

    mats_there = flipped(transfer[1], "bfly", 2)
    mats = prepare(transfer, partner_perm, 0)
    there = prepare(mats_there[None], partner_perm, 1)

    def chain(n, bases):
        j, at, width = CHUNKS[n]
        own = project(obs_field, bases, j, at, width)
        near = yield own, flipped(own, "obs", 1)
        sent = jnp.where(pass_on, near, own)
        far = yield sent, flipped(sent, "obs", 3)
        c = jnp.where(stays, own, jnp.where(from_near, near, far))
        p = yield c, flipped(c, "bfly", 1)
        c = step(c, p, mats, 0, j)
        p = yield c, flipped(c, "bfly", 2)
        d = step(p, c, there, 0, j)
        q = yield d, flipped(d, "bfly", 6)
        c = step(c, p, mats, 1, j)
        c = step(c, q, mats, 2, j)
        p = yield c, flipped(c, "bfly", 8)
        c = step(c, p, mats, 3, j)
        top, end = c[: 2 * width], c[2 * width :]
        sent = jnp.where(outer, end, top)
        got = yield sent, flipped(sent, "obs", 1)
        c = jnp.where(outer, top, end) + got
        top, end = c[:width], c[width:]
        sent = jnp.where(inner, end, top)
        got = yield sent, flipped(sent, "obs", 3)
        c = jnp.where(inner, top, end) + got
        out = lax.dot_general(
            c, src_basis[j], NT, precision=lax.Precision.HIGHEST,
            preferred_element_type=jnp.float32,
        )
        yield out, out

    chains = {}
    waiting = {}
    last = None
    for n in ORDER:
        if n not in chains:
            bases = observer_leaf_bases
            if last is not None:
                bases, _ = lax.optimization_barrier((bases, last))
            chains[n] = chain(n, bases)
            last, waiting[n] = next(chains[n])
        else:
            value, _ = lax.optimization_barrier((waiting[n], last))
            last, waiting[n] = chains[n].send(value)
    rows = {}
    for n, (node, at, width) in enumerate(CHUNKS):
        rows.setdefault(node, {})[at] = waiting[n]
    return jnp.concatenate(
        [
            jnp.concatenate([rows[node][at] for at in sorted(rows[node])], 0)
            for node in range(nodes)
        ],
        1,
    )


def solution(mesh):
    placed = (
        P(("obs", "bfly"), None),
        P(("obs", "bfly"), None, None),
        P(None, ("obs", "bfly"), None, None),
        P("bfly", None, None),
        P(),
        P(),
    )
    return jax.shard_map(
        body, mesh=mesh, in_specs=placed, out_specs=P("obs", "bfly"), check_vma=False
    )
```

```python
import functools

import jax
import jax.numpy as jnp
from jax import lax
from jax.experimental import pallas as pl
from jax.experimental.pallas import tpu as pltpu
from jax.sharding import PartitionSpec as P

CHUNKS = ((0, 0, 128), (0, 128, 128), (1, 0, 128), (1, 128, 128))
ORDER = (0, 1, 2, 3, 0, 1, 0, 2, 1, 0, 3, 2, 1, 0, 3, 2, 1, 0, 3, 2, 1, 0, 3, 2, 1, 0, 3, 2, 1, 0, 3, 2, 1, 3, 2, 3)
LIMIT = 12 << 20
CHEAP = pl.CostEstimate(flops=0, transcendentals=0, bytes_accessed=0)
NT = (((1,), (1,)), ((), ()))
TN = (((0,), (0,)), ((), ()))


def flipped(block, axis, mask):
    count = lax.axis_size(axis)
    return lax.ppermute(block, axis, [(i, i ^ mask) for i in range(count)])


def halves(block):
    high = block.astype(jnp.bfloat16)
    return high, (block - high.astype(jnp.float32)).astype(jnp.bfloat16)


def dot(a, b, dims):
    return lax.dot_general(a, b, dims, preferred_element_type=jnp.float32)


def dot3(a, b, dims):
    (ah, al), (bh, bl) = a, b
    return dot(ah, bh, dims) + (dot(ah, bl, dims) + dot(al, bh, dims))


def choose_kernel(leaf_map, out):
    x = lax.axis_index("obs")
    b = lax.axis_index("bfly")
    at = lax.broadcasted_iota(jnp.int32, (1, leaf_map.shape[1]), 1)
    turn = jnp.sum(jnp.where(at == b, leaf_map[0:1, :], 0), axis=1, keepdims=True)
    turn = jnp.broadcast_to(turn, (1, out.shape[1]))
    out[0:1, :] = turn ^ 2
    out[1:2, :] = turn
    out[2:3, :] = (x + turn) % 4 ^ x ^ 1
    out[3:4, :] = jnp.zeros_like(turn) + (x ^ x >> 1) % 2
    out[4:5, :] = jnp.zeros_like(turn) + x % 2


def choose(leaf_map, width):
    return pl.pallas_call(
        choose_kernel,
        grid=(1,),
        in_specs=[pl.BlockSpec(leaf_map.shape, lambda i: (0, 0))],
        out_specs=pl.BlockSpec((8, width), lambda i: (0, 0)),
        out_shape=jax.ShapeDtypeStruct((8, width), jnp.int32),
        compiler_params=pltpu.CompilerParams(vmem_limit_bytes=1 << 20),
        cost_estimate=CHEAP,
    )(leaf_map)


def project_kernel(block, basis, out, high, low):
    @pl.when(pl.program_id(0) == 0)
    def _():
        high[...], low[...] = halves(basis[0])

    out[...] = dot3(halves(block[...]), (high[...], low[...]), TN)


def project(obs_field, bases, node, at, width):
    nodes, leaf, rank = bases.shape
    share = obs_field.shape[1] // 4
    return pl.pallas_call(
        project_kernel,
        grid=(4,),
        in_specs=[
            pl.BlockSpec(
                (leaf, width), lambda i: (node, (3 * i) % 4 * (share // width) + at // width)
            ),
            pl.BlockSpec((1, leaf, rank), lambda i: (node, 0, 0)),
        ],
        out_specs=pl.BlockSpec((width, rank), lambda i: (i, 0)),
        out_shape=jax.ShapeDtypeStruct((4 * width, rank), jnp.float32),
        scratch_shapes=[pltpu.VMEM((leaf, rank), jnp.bfloat16)] * 2,
        compiler_params=pltpu.CompilerParams(vmem_limit_bytes=LIMIT),
        cost_estimate=CHEAP,
    )(obs_field, bases)


def prepare_kernel(first, perm, mats, high, low):
    rank = mats.shape[2]
    h, l = halves(mats[0, 0])
    row = perm[pl.ds(first + pl.program_id(0), 1), :]
    picks = lax.broadcasted_iota(jnp.int32, (rank, rank), 0)
    onehot = (row == picks).astype(jnp.bfloat16)
    dims = NT
    for out, part in ((high, h), (low, l)):
        out[0, 0, :, :rank] = part[:, :rank]
        out[0, 0, :, rank:] = dot(part[:, rank:], onehot, dims).astype(jnp.bfloat16)


def prepare(mats, perm, first):
    levels, nodes, rank, two = mats.shape
    spec = pl.BlockSpec((1, 1, rank, two), lambda k, j: (k, j, 0, 0))
    return pl.pallas_call(
        functools.partial(prepare_kernel, first),
        grid=(levels, nodes),
        in_specs=[pl.BlockSpec(perm.shape, lambda k, j: (0, 0)), spec],
        out_specs=[spec, spec],
        out_shape=[jax.ShapeDtypeStruct(mats.shape, jnp.bfloat16)] * 2,
        compiler_params=pltpu.CompilerParams(vmem_limit_bytes=LIMIT),
        cost_estimate=CHEAP,
    )(perm, mats)


def step_kernel(a, b, high, low, out):
    rank = a.shape[1]
    h, l = high[0, 0], low[0, 0]
    out[...] = dot3(halves(a[...]), (h[:, :rank], l[:, :rank]), NT) + dot3(
        halves(b[...]), (h[:, rank:], l[:, rank:]), NT
    )


def step(a, b, mats, k, j):
    whole = pl.BlockSpec(a.shape, lambda i: (0, 0))
    one = pl.BlockSpec((1, 1) + mats[0].shape[2:], lambda i: (k, j, 0, 0))
    return pl.pallas_call(
        step_kernel,
        grid=(1,),
        in_specs=[whole, whole, one, one],
        out_specs=whole,
        out_shape=jax.ShapeDtypeStruct(a.shape, jnp.float32),
        compiler_params=pltpu.CompilerParams(vmem_limit_bytes=LIMIT),
        cost_estimate=CHEAP,
    )(a, b, *mats)


def body(obs_field, observer_leaf_bases, transfer, src_basis, leaf_map, partner_perm):
    nodes, leaf, rank = observer_leaf_bases.shape
    obs_field = pltpu.with_memory_space_constraint(obs_field, pltpu.HBM)
    picks = choose(leaf_map, rank)

    def where(k, a, b):
        return jnp.where(picks[k : k + 1] == 0, a, b)

    mats_there = flipped(transfer[1], "bfly", 2)
    mats = prepare(transfer, partner_perm, 0)
    there = prepare(mats_there[None], partner_perm, 1)

    def chain(n, bases):
        j, at, width = CHUNKS[n]
        own = project(obs_field, bases, j, at, width)
        near = yield own, flipped(own, "obs", 1)
        sent = where(0, near, own)
        far = yield sent, flipped(sent, "obs", 3)
        c = where(1, own, where(2, near, far))
        p = yield c, flipped(c, "bfly", 1)
        c = step(c, p, mats, 0, j)
        p = yield c, flipped(c, "bfly", 2)
        d = step(p, c, there, 0, j)
        q = yield d, flipped(d, "bfly", 6)
        c = step(c, p, mats, 1, j)
        c = step(c, q, mats, 2, j)
        p = yield c, flipped(c, "bfly", 8)
        c = step(c, p, mats, 3, j)
        top, end = c[: 2 * width], c[2 * width :]
        sent = where(3, end, top)
        got = yield sent, flipped(sent, "obs", 1)
        c = where(3, top, end) + got
        top, end = c[:width], c[width:]
        sent = where(4, end, top)
        got = yield sent, flipped(sent, "obs", 3)
        c = where(4, top, end) + got
        out = lax.dot_general(
            c, src_basis[j], NT, precision=lax.Precision.HIGHEST,
            preferred_element_type=jnp.float32,
        )
        yield out, out

    chains = {}
    waiting = {}
    last = None
    for n in ORDER:
        if n not in chains:
            bases = observer_leaf_bases
            if last is not None:
                bases, _ = lax.optimization_barrier((bases, last))
            chains[n] = chain(n, bases)
            last, waiting[n] = next(chains[n])
        else:
            value, _ = lax.optimization_barrier((waiting[n], last))
            last, waiting[n] = chains[n].send(value)
    rows = {}
    for n, (node, at, width) in enumerate(CHUNKS):
        rows.setdefault(node, {})[at] = waiting[n]
    return jnp.concatenate(
        [
            jnp.concatenate([rows[node][at] for at in sorted(rows[node])], 0)
            for node in range(nodes)
        ],
        1,
    )


def solution(mesh):
    placed = (
        P(("obs", "bfly"), None),
        P(("obs", "bfly"), None, None),
        P(None, ("obs", "bfly"), None, None),
        P("bfly", None, None),
        P(),
        P(),
    )
    return jax.shard_map(
        body, mesh=mesh, in_specs=placed, out_specs=P("obs", "bfly"), check_vma=False
    )
```

```python
import functools

import jax
import jax.numpy as jnp
from jax import lax
from jax.experimental import pallas as pl
from jax.experimental.pallas import tpu as pltpu
from jax.sharding import PartitionSpec as P

CHUNKS = ((0, 0, 128), (0, 128, 128), (1, 0, 128), (1, 128, 128))
ORDER = (0, 1, 2, 3, 0, 1, 0, 2, 1, 0, 3, 2, 1, 0, 3, 2, 1, 0, 3, 2, 1, 0, 3, 2, 1, 0, 3, 2, 1, 0, 3, 2, 1, 3, 2, 3)
LIMIT = 12 << 20
CHEAP = pl.CostEstimate(flops=0, transcendentals=0, bytes_accessed=0)
NT = (((1,), (1,)), ((), ()))
TN = (((0,), (0,)), ((), ()))


def flipped(block, axis, mask):
    count = lax.axis_size(axis)
    return lax.ppermute(block, axis, [(i, i ^ mask) for i in range(count)])


def halves(block):
    high = block.astype(jnp.bfloat16)
    return high, (block - high.astype(jnp.float32)).astype(jnp.bfloat16)


def dot(a, b, dims):
    return lax.dot_general(a, b, dims, preferred_element_type=jnp.float32)


def dot3(a, b, dims):
    (ah, al), (bh, bl) = a, b
    return dot(ah, bh, dims) + (dot(ah, bl, dims) + dot(al, bh, dims))


def choose_kernel(leaf_map, out):
    x = lax.axis_index("obs")
    b = lax.axis_index("bfly")
    at = lax.broadcasted_iota(jnp.int32, (1, leaf_map.shape[1]), 1)
    turn = jnp.sum(jnp.where(at == b, leaf_map[0:1, :], 0), axis=1, keepdims=True)
    turn = jnp.broadcast_to(turn, (1, out.shape[1]))
    out[0:1, :] = turn ^ 2
    out[1:2, :] = turn
    out[2:3, :] = (x + turn) % 4 ^ x ^ 1
    out[3:4, :] = jnp.zeros_like(turn) + (x ^ x >> 1) % 2
    out[4:5, :] = jnp.zeros_like(turn) + x % 2


def choose(leaf_map, width):
    return pl.pallas_call(
        choose_kernel,
        grid=(1,),
        in_specs=[pl.BlockSpec(leaf_map.shape, lambda i: (0, 0))],
        out_specs=pl.BlockSpec((8, width), lambda i: (0, 0)),
        out_shape=jax.ShapeDtypeStruct((8, width), jnp.int32),
        compiler_params=pltpu.CompilerParams(vmem_limit_bytes=1 << 20),
        cost_estimate=CHEAP,
    )(leaf_map)


def project_kernel(*refs):
    *blocks, basis, out = refs
    width = blocks[0].shape[1]
    split = halves(basis[0])
    for i, block in enumerate(blocks):
        out[i * width : (i + 1) * width, :] = dot3(halves(block[...]), split, TN)


def project(obs_field, bases, node, at, width):
    nodes, leaf, rank = bases.shape
    share = obs_field.shape[1] // 4
    bases = pltpu.with_memory_space_constraint(bases, pltpu.HBM)
    columns = [
        pl.BlockSpec(
            (leaf, width), functools.partial(lambda k, i: (node, k), (q * share + at) // width)
        )
        for q in (0, 3, 2, 1)
    ]
    return pl.pallas_call(
        project_kernel,
        grid=(1,),
        in_specs=columns + [pl.BlockSpec((1, leaf, rank), lambda i: (node, 0, 0))],
        out_specs=pl.BlockSpec((4 * width, rank), lambda i: (0, 0)),
        out_shape=jax.ShapeDtypeStruct((4 * width, rank), jnp.float32),
        compiler_params=pltpu.CompilerParams(vmem_limit_bytes=LIMIT),
        cost_estimate=CHEAP,
    )(*[obs_field] * 4, bases)


def prepare_kernel(first, perm, mats, high, low):
    rank = mats.shape[2]
    h, l = halves(mats[0, 0])
    row = perm[pl.ds(first + pl.program_id(0), 1), :]
    picks = lax.broadcasted_iota(jnp.int32, (rank, rank), 0)
    onehot = (row == picks).astype(jnp.bfloat16)
    dims = NT
    for out, part in ((high, h), (low, l)):
        out[0, 0, :, :rank] = part[:, :rank]
        out[0, 0, :, rank:] = dot(part[:, rank:], onehot, dims).astype(jnp.bfloat16)


def prepare(mats, perm, first):
    levels, nodes, rank, two = mats.shape
    spec = pl.BlockSpec((1, 1, rank, two), lambda k, j: (k, j, 0, 0))
    return pl.pallas_call(
        functools.partial(prepare_kernel, first),
        grid=(levels, nodes),
        in_specs=[pl.BlockSpec(perm.shape, lambda k, j: (0, 0)), spec],
        out_specs=[spec, spec],
        out_shape=[jax.ShapeDtypeStruct(mats.shape, jnp.bfloat16)] * 2,
        compiler_params=pltpu.CompilerParams(vmem_limit_bytes=LIMIT),
        cost_estimate=CHEAP,
    )(perm, mats)


def step_kernel(a, b, high, low, out):
    rank = a.shape[1]
    h, l = high[0, 0], low[0, 0]
    out[...] = dot3(halves(a[...]), (h[:, :rank], l[:, :rank]), NT) + dot3(
        halves(b[...]), (h[:, rank:], l[:, rank:]), NT
    )


def step(a, b, mats, k, j):
    whole = pl.BlockSpec(a.shape, lambda i: (0, 0))
    one = pl.BlockSpec((1, 1) + mats[0].shape[2:], lambda i: (k, j, 0, 0))
    return pl.pallas_call(
        step_kernel,
        grid=(1,),
        in_specs=[whole, whole, one, one],
        out_specs=whole,
        out_shape=jax.ShapeDtypeStruct(a.shape, jnp.float32),
        compiler_params=pltpu.CompilerParams(vmem_limit_bytes=LIMIT),
        cost_estimate=CHEAP,
    )(a, b, *mats)


def body(obs_field, observer_leaf_bases, transfer, src_basis, leaf_map, partner_perm):
    nodes, leaf, rank = observer_leaf_bases.shape
    obs_field = pltpu.with_memory_space_constraint(obs_field, pltpu.HBM)
    picks = choose(leaf_map, rank)

    def where(k, a, b):
        return jnp.where(picks[k : k + 1] == 0, a, b)

    mats_there = flipped(transfer[1], "bfly", 2)
    mats = prepare(transfer, partner_perm, 0)
    there = prepare(mats_there[None], partner_perm, 1)

    def chain(n, bases):
        j, at, width = CHUNKS[n]
        own = project(obs_field, bases, j, at, width)
        near = yield own, flipped(own, "obs", 1)
        sent = where(0, near, own)
        far = yield sent, flipped(sent, "obs", 3)
        c = where(1, own, where(2, near, far))
        p = yield c, flipped(c, "bfly", 1)
        c = step(c, p, mats, 0, j)
        p = yield c, flipped(c, "bfly", 2)
        d = step(p, c, there, 0, j)
        q = yield d, flipped(d, "bfly", 6)
        c = step(c, p, mats, 1, j)
        c = step(c, q, mats, 2, j)
        p = yield c, flipped(c, "bfly", 8)
        c = step(c, p, mats, 3, j)
        top, end = c[: 2 * width], c[2 * width :]
        sent = where(3, end, top)
        got = yield sent, flipped(sent, "obs", 1)
        c = where(3, top, end) + got
        top, end = c[:width], c[width:]
        sent = where(4, end, top)
        got = yield sent, flipped(sent, "obs", 3)
        c = where(4, top, end) + got
        out = lax.dot_general(
            c, src_basis[j], NT, precision=lax.Precision.HIGHEST,
            preferred_element_type=jnp.float32,
        )
        yield out, out

    chains = {}
    waiting = {}
    last = None
    for n in ORDER:
        if n not in chains:
            bases = observer_leaf_bases
            if last is not None:
                bases, _ = lax.optimization_barrier((bases, last))
            chains[n] = chain(n, bases)
            last, waiting[n] = next(chains[n])
        else:
            value, _ = lax.optimization_barrier((waiting[n], last))
            last, waiting[n] = chains[n].send(value)
    rows = {}
    for n, (node, at, width) in enumerate(CHUNKS):
        rows.setdefault(node, {})[at] = waiting[n]
    return jnp.concatenate(
        [
            jnp.concatenate([rows[node][at] for at in sorted(rows[node])], 0)
            for node in range(nodes)
        ],
        1,
    )


def solution(mesh):
    placed = (
        P(("obs", "bfly"), None),
        P(("obs", "bfly"), None, None),
        P(None, ("obs", "bfly"), None, None),
        P("bfly", None, None),
        P(),
        P(),
    )
    return jax.shard_map(
        body, mesh=mesh, in_specs=placed, out_specs=P("obs", "bfly"), check_vma=False
    )
```

```python
import functools

import jax
import jax.numpy as jnp
from jax import lax
from jax.experimental import pallas as pl
from jax.experimental.pallas import tpu as pltpu
from jax.sharding import PartitionSpec as P

CHUNKS = ((0, 0, 128), (0, 128, 128), (1, 0, 128), (1, 128, 128))
ORDER = (0, 1, 2, 3, 0, 1, 0, 2, 1, 0, 3, 2, 1, 0, 3, 2, 1, 0, 3, 2, 1, 0, 3, 2, 1, 0, 3, 2, 1, 0, 3, 2, 1, 3, 2, 3)
LIMIT = 12 << 20
CHEAP = pl.CostEstimate(flops=0, transcendentals=0, bytes_accessed=0)
NT = (((1,), (1,)), ((), ()))
TN = (((0,), (0,)), ((), ()))


def flipped(block, axis, mask):
    count = lax.axis_size(axis)
    return lax.ppermute(block, axis, [(i, i ^ mask) for i in range(count)])


def halves(block):
    high = block.astype(jnp.bfloat16)
    return high, (block - high.astype(jnp.float32)).astype(jnp.bfloat16)


def dot(a, b, dims):
    return lax.dot_general(a, b, dims, preferred_element_type=jnp.float32)


def dot3(a, b, dims):
    (ah, al), (bh, bl) = a, b
    return dot(ah, bh, dims) + (dot(ah, bl, dims) + dot(al, bh, dims))


def choose_kernel(leaf_map, out):
    x = lax.axis_index("obs")
    b = lax.axis_index("bfly")
    at = lax.broadcasted_iota(jnp.int32, (1, leaf_map.shape[1]), 1)
    turn = jnp.sum(jnp.where(at == b, leaf_map[0:1, :], 0), axis=1, keepdims=True)
    turn = jnp.broadcast_to(turn, (1, out.shape[1]))
    out[0:1, :] = turn ^ 2
    out[1:2, :] = turn
    out[2:3, :] = (x + turn) % 4 ^ x ^ 1
    out[3:4, :] = jnp.zeros_like(turn) + (x ^ x >> 1) % 2
    out[4:5, :] = jnp.zeros_like(turn) + x % 2


def choose(leaf_map, width):
    return pl.pallas_call(
        choose_kernel,
        grid=(1,),
        in_specs=[pl.BlockSpec(leaf_map.shape, lambda i: (0, 0))],
        out_specs=pl.BlockSpec((8, width), lambda i: (0, 0)),
        out_shape=jax.ShapeDtypeStruct((8, width), jnp.int32),
        compiler_params=pltpu.CompilerParams(vmem_limit_bytes=1 << 20),
        cost_estimate=CHEAP,
    )(leaf_map)


def project_kernel(*refs):
    *blocks, basis, out = refs
    width = blocks[0].shape[1]
    split = halves(basis[0])
    for i, block in enumerate(blocks):
        out[i * width : (i + 1) * width, :] = dot3(halves(block[...]), split, TN)


def project(obs_field, bases, node, at, width):
    nodes, leaf, rank = bases.shape
    share = obs_field.shape[1] // 4
    bases = pltpu.with_memory_space_constraint(bases, pltpu.HBM)
    columns = [
        pl.BlockSpec(
            (leaf, width), functools.partial(lambda k, i: (node, k), (q * share + at) // width)
        )
        for q in (0, 3, 2, 1)
    ]
    return pl.pallas_call(
        project_kernel,
        grid=(1,),
        in_specs=columns + [pl.BlockSpec((1, leaf, rank), lambda i: (node, 0, 0))],
        out_specs=pl.BlockSpec((4 * width, rank), lambda i: (0, 0)),
        out_shape=jax.ShapeDtypeStruct((4 * width, rank), jnp.float32),
        compiler_params=pltpu.CompilerParams(vmem_limit_bytes=LIMIT),
        cost_estimate=CHEAP,
    )(*[obs_field] * 4, bases)


def prepare_kernel(first, perm, mats, high, low):
    rank = mats.shape[2]
    h, l = halves(mats[0, 0])
    row = perm[pl.ds(first + pl.program_id(0), 1), :]
    picks = lax.broadcasted_iota(jnp.int32, (rank, rank), 0)
    onehot = (row == picks).astype(jnp.bfloat16)
    dims = NT
    for out, part in ((high, h), (low, l)):
        out[0, 0, :, :rank] = part[:, :rank]
        out[0, 0, :, rank:] = dot(part[:, rank:], onehot, dims).astype(jnp.bfloat16)


def prepare(mats, perm, first):
    levels, nodes, rank, two = mats.shape
    spec = pl.BlockSpec((1, 1, rank, two), lambda k, j: (k, j, 0, 0))
    return pl.pallas_call(
        functools.partial(prepare_kernel, first),
        grid=(levels, nodes),
        in_specs=[pl.BlockSpec(perm.shape, lambda k, j: (0, 0)), spec],
        out_specs=[spec, spec],
        out_shape=[jax.ShapeDtypeStruct(mats.shape, jnp.bfloat16)] * 2,
        compiler_params=pltpu.CompilerParams(vmem_limit_bytes=LIMIT),
        cost_estimate=CHEAP,
    )(perm, mats)


def step_kernel(a, b, high, low, out):
    rank = a.shape[1]
    h, l = high[0, 0], low[0, 0]
    out[...] = dot3(halves(a[...]), (h[:, :rank], l[:, :rank]), NT) + dot3(
        halves(b[...]), (h[:, rank:], l[:, rank:]), NT
    )


def step(a, b, mats, k, j):
    whole = pl.BlockSpec(a.shape, lambda i: (0, 0))
    one = pl.BlockSpec((1, 1) + mats[0].shape[2:], lambda i: (k, j, 0, 0))
    return pl.pallas_call(
        step_kernel,
        grid=(1,),
        in_specs=[whole, whole, one, one],
        out_specs=whole,
        out_shape=jax.ShapeDtypeStruct(a.shape, jnp.float32),
        compiler_params=pltpu.CompilerParams(vmem_limit_bytes=LIMIT),
        cost_estimate=CHEAP,
    )(a, b, *mats)


def expand_kernel(src, *refs):
    *blocks, out = refs
    n = pl.program_id(0) * 2 + pl.program_id(1)
    for k, block in enumerate(blocks):

        @pl.when(n == k)
        def _():
            out[...] = dot3(halves(block[...]), halves(src[0]), NT)


def expand(blocks, src_basis):
    nodes, leaf, rank = src_basis.shape
    width = blocks[0].shape[0]
    return pl.pallas_call(
        expand_kernel,
        grid=(nodes, 2),
        in_specs=[pl.BlockSpec((1, leaf, rank), lambda j, h: (j, 0, 0))]
        + [pl.BlockSpec(block.shape, lambda j, h: (0, 0)) for block in blocks],
        out_specs=pl.BlockSpec((width, leaf), lambda j, h: (h, j)),
        out_shape=jax.ShapeDtypeStruct((2 * width, nodes * leaf), jnp.float32),
        compiler_params=pltpu.CompilerParams(vmem_limit_bytes=LIMIT),
        cost_estimate=CHEAP,
    )(src_basis, *blocks)


def body(obs_field, observer_leaf_bases, transfer, src_basis, leaf_map, partner_perm):
    nodes, leaf, rank = observer_leaf_bases.shape
    obs_field = pltpu.with_memory_space_constraint(obs_field, pltpu.HBM)
    picks = choose(leaf_map, rank)

    def where(k, a, b):
        return jnp.where(picks[k : k + 1] == 0, a, b)

    mats_there = flipped(transfer[1], "bfly", 2)
    mats = prepare(transfer, partner_perm, 0)
    there = prepare(mats_there[None], partner_perm, 1)

    def chain(n, bases):
        j, at, width = CHUNKS[n]
        own = project(obs_field, bases, j, at, width)
        near = yield own, flipped(own, "obs", 1)
        sent = where(0, near, own)
        far = yield sent, flipped(sent, "obs", 3)
        c = where(1, own, where(2, near, far))
        p = yield c, flipped(c, "bfly", 1)
        c = step(c, p, mats, 0, j)
        p = yield c, flipped(c, "bfly", 2)
        d = step(p, c, there, 0, j)
        q = yield d, flipped(d, "bfly", 6)
        c = step(c, p, mats, 1, j)
        c = step(c, q, mats, 2, j)
        p = yield c, flipped(c, "bfly", 8)
        c = step(c, p, mats, 3, j)
        top, end = c[: 2 * width], c[2 * width :]
        sent = where(3, end, top)
        got = yield sent, flipped(sent, "obs", 1)
        c = where(3, top, end) + got
        top, end = c[:width], c[width:]
        sent = where(4, end, top)
        got = yield sent, flipped(sent, "obs", 3)
        c = where(4, top, end) + got
        yield c, c

    chains = {}
    waiting = {}
    last = None
    for n in ORDER:
        if n not in chains:
            bases = observer_leaf_bases
            if last is not None:
                bases, _ = lax.optimization_barrier((bases, last))
            chains[n] = chain(n, bases)
            last, waiting[n] = next(chains[n])
        else:
            value, _ = lax.optimization_barrier((waiting[n], last))
            last, waiting[n] = chains[n].send(value)
    return expand([waiting[n] for n in range(len(CHUNKS))], src_basis)


def solution(mesh):
    placed = (
        P(("obs", "bfly"), None),
        P(("obs", "bfly"), None, None),
        P(None, ("obs", "bfly"), None, None),
        P("bfly", None, None),
        P(),
        P(),
    )
    return jax.shard_map(
        body, mesh=mesh, in_specs=placed, out_specs=P("obs", "bfly"), check_vma=False
    )
```
